32 devices in a mesh: expert: 4 (over y, x), dp: 8 (over z, core).
Axes of the slice: x: 2, y: 2, z: 4, core: 2. Of those that a mesh axis runs over, the one named last changes fastest.
Arguments:
- tokens: bfloat16 [512, 3072], P(('expert', 'dp')), may hold values from -6 to 6
- cotangent: bfloat16 [512, 3072], P(('expert', 'dp')), may hold values from -6 to 6
- experts: int32 [512, 2], P(('expert', 'dp')), may hold values from 0 to 3, all different within a row; in each aligned block of 16 rows (0 to 15, 16 to 31, ...) at most 8 rows name the same one
- gate_weights: float32 [512, 2], P(('expert', 'dp')), may hold values from 0.1 to 1
- w_up: bfloat16 [4, 3072, 8192], P('expert', None, 'dp'), may hold values from -0.109375 to 0.109375
- master: float32 [4, 8192, 3072], P(None, 'dp', 'expert'), may hold values from -6 to 6
- moment_one: bfloat16 [4, 8192, 3072], P(None, 'dp', 'expert'), may hold values from -18 to 18
- moment_two: bfloat16 [4, 8192, 3072], P(None, 'dp', 'expert'), may hold values from 10 to 100
Outputs:
- new_master: float32 [4, 8192, 3072], P('expert', 'dp')
The draws below stay inside these ranges and needn't reach their ends.
Inputs may be any that keep to these rules, and one draw needn't show every extreme that they name: Each token names two different experts; the tokens of one device name any expert at most 8 times, a bound that some block reaches.
All inputs are finite; a program needn't handle non-finite values.
Results may differ from the reference program's by a relative error of at most 0.0003.
Values may be sent and summed in bfloat16 or wider, within the bound.
No kernel may reach another device: no remote copies, remote signals or barrier semaphores. Data moves between devices by JAX's collectives and lax.ppermute only.
A program may use at most 192 MiB of HBM per device.

```python
import math
import jax
import jax.numpy as jnp
import numpy as np
from jax import lax

D = 3072
F = 8192
E = 4
TOK_DEV = 16
CAP = 8
TOKENS = 512
DEVICES = 32


def steps_of(rng, extent, pieces, least, largest):
    gain = 1.0
    for dim, blocks in pieces:
        steps = jax.random.uniform(jax.random.fold_in(jax.random.fold_in(rng, 6), dim), (blocks,), jnp.float32, least / len(pieces), largest / len(pieces))
        gain = gain * jnp.repeat(jnp.exp(steps), extent[dim] // blocks).reshape((-1,) + (1,) * (len(extent) - 1 - dim))
    return gain


def routed_block(key, own, number, rows, amount, top, limit, slope):
    sequence = jax.random.permutation(key, amount)
    packed, usual = shares(amount, rows * top, limit, slope, True), shares(amount, rows * top, limit, slope, False)
    places = jnp.arange(amount)

    def named(sizes, offset_by):
        used = int((sizes > 0).sum())
        fixed = max(1, used // 4)
        moved = fixed + (places - fixed + offset_by * (used - fixed)) % max(1, amount - fixed)
        return jnp.zeros((amount,), jnp.int32).at[sequence[jnp.where(places < fixed, places, moved)]].set(jnp.asarray(sizes, jnp.int32))

    sizes = jnp.where(number % 4 == 0, named(packed, number // 4), named(usual, number - number // 4 - 1))
    mixed = jax.random.permutation(jax.random.fold_in(own, 3), amount)
    donor, sink = mixed[0:amount // 2 * 2:2], mixed[1:amount // 2 * 2:2]
    room = jnp.minimum(sizes[donor] - 1, limit - sizes[sink]) // 2
    room = jnp.where((donor == sequence[0]) | (sink == sequence[0]) | (sizes[sink] == 0), 0, jnp.maximum(room, 0))
    moved = jax.random.randint(jax.random.fold_in(own, 4), (amount // 2,), 0, 1 << 20) % (room + 1)
    sizes = sizes.at[donor].add(-moved).at[sink].add(moved)
    items = jnp.searchsorted(jnp.cumsum(sizes), jnp.arange(rows * top), side="right").astype(jnp.int32)
    grid = items.reshape(top, rows).T
    grid = grid[jax.random.permutation(jax.random.fold_in(own, 1), rows)]
    offset_by = jax.random.randint(jax.random.fold_in(own, 2), (rows, 1), 0, top)
    return jnp.take_along_axis(grid, (jnp.arange(top)[None, :] + offset_by) % top, axis=1)


def shares(amount, total, most, slope, full):
    weights = [(1 << 20) // math.isqrt(standing ** slope) + 1 for standing in range(1, amount + 1)]
    largest = most if full else min(most, max(-(-total // amount), total * weights[0] // sum(weights)))
    least = 1 if total - largest >= amount - 1 else 0
    holding, surplus = [largest] + [least] * (amount - 1), total - largest - least * (amount - 1)
    while surplus > 0:
        candidates = [i for i in range(1, amount) if holding[i] < largest] or [i for i in range(1, amount) if holding[i] < most]
        whole, budget = sum([weights[i] for i in candidates]), surplus
        for i in candidates:
            addition = min(most - holding[i], max(1, budget * weights[i] // whole), surplus)
            holding[i] = holding[i] + addition
            surplus = surplus - addition
    return np.array(holding)


def scatter_about(own_key, shape, deviation, most, pieces=(), kind=jnp.bfloat16):
    array = deviation * jax.random.normal(own_key, shape, jnp.float32)
    if pieces:
        array = array * steps_of(own_key, shape, pieces, -0.22, 0.18)
    return jnp.clip(array, -most, most).astype(kind)


def setup_inputs(seed: int = 0) -> dict:
    splits = jax.random.split(jax.random.key(seed), 9)
    tokens = scatter_about(splits[0], (TOKENS, D), 1.0, 6.0, ((0, 32),))
    cotangent = scatter_about(splits[1], (TOKENS, D), 1.0, 6.0, ((0, 32),))
    experts_keys = jax.random.split(jax.random.fold_in(splits[2], 1), TOKENS // TOK_DEV)
    experts_turns = jax.random.permutation(jax.random.fold_in(splits[2], 3), TOKENS // TOK_DEV)
    experts = jax.vmap(lambda own, number: routed_block(jax.random.fold_in(splits[2], 2), own, number, TOK_DEV, E, 2, CAP, 2))(experts_keys, experts_turns).reshape((TOKENS, 2))
    gate_weights = jnp.clip(0.1 + 0.9 * jax.random.uniform(splits[3], (TOKENS, 2), jnp.float32) ** steps_of(splits[3], (TOKENS, 2), ((0, 32),), -0.2, 0.2), 0.1, 1.0)
    w_up = scatter_about(splits[4], (E, D, F), D ** -0.5, 0.109375, ((0, 4), (2, 8)))
    master = scatter_about(splits[5], (E, F, D), 1.0, 6.0, ((1, 8), (2, 4)), jnp.float32)
    moment_one = scatter_about(splits[6], (E, F, D), 3.0, 18.0, ((1, 8), (2, 4)))
    moment_two = jnp.clip(jnp.exp(math.log(100.0) - 2.3025851 * jax.random.uniform(splits[7], (E, F, D), jnp.float32) ** steps_of(splits[7], (E, F, D), ((1, 8), (2, 4)), -0.2, 0.2)), 10.0, 100.0).astype(jnp.bfloat16)
    return dict(tokens=tokens, cotangent=cotangent, experts=experts, gate_weights=gate_weights, w_up=w_up, master=master, moment_one=moment_one, moment_two=moment_two)


beta_one = 0.9
beta_two = 0.95
corr_one = 1.0 - (0.9 ** 50) ** 2
corr_two = 1.0 - (0.95 ** 50) ** 2
learn_rate = 0.2
weight_decay = 0.1
epsilon = 1e-08

def reference(tokens, cotangent, experts, gate_weights, w_up, master, moment_one, moment_two):
    row_count = DEVICES * CAP

    def per_expert(expert_index):
        matched = experts == expert_index
        weight = lax.optimization_barrier(jnp.sum(jnp.where(matched, gate_weights, jnp.float32(0.0)), axis=1))
        chosen = jnp.any(matched, axis=1)
        sort_key = jnp.where(chosen, 0, 1).astype(jnp.int32)
        picked = jnp.argsort(sort_key, stable=True)[:row_count].astype(jnp.int32)
        is_live = chosen[picked]
        scaled = (cotangent[picked].astype(jnp.float32) * weight[picked][:, None]).astype(jnp.bfloat16)
        scaled = jnp.where(is_live[:, None], scaled, jnp.zeros_like(scaled))
        hidden = jax.nn.silu(jnp.dot(tokens[picked], w_up[expert_index], preferred_element_type=jnp.float32)).astype(jnp.bfloat16)
        return lax.dot_general(hidden, scaled, (((0,), (0,)), ((), ())), preferred_element_type=jnp.float32)
    gradient = lax.map(per_expert, jnp.arange(E, dtype=jnp.int32))
    first = beta_one * moment_one.astype(jnp.float32) + (1.0 - beta_one) * gradient
    second = beta_two * moment_two.astype(jnp.float32) + (1.0 - beta_two) * gradient * gradient
    update = first / corr_one / (jnp.sqrt(second / corr_two) + epsilon)
    return master - learn_rate * (update + weight_decay * master)
```

```python
import functools

import jax
import jax.numpy as jnp
from jax import lax
from jax.experimental import pallas as pl
from jax.experimental.pallas import tpu as pltpu
from jax.sharding import PartitionSpec as P

CAP = 8
LANES = 128
TILE = 16
TOP = 32767.0
FLOOR = 1e-30

beta_one = 0.9
beta_two = 0.95
corr_one = 1.0 - (0.9**50) ** 2
corr_two = 1.0 - (0.95**50) ** 2
learn_rate = 0.2
weight_decay = 0.1
epsilon = 1e-08

f32 = jnp.float32
bf16 = jnp.bfloat16
VMEM = pl.BlockSpec(memory_space=pltpu.VMEM)


def adam_update(master, moment_one, moment_two, gradient):
    first = beta_one * moment_one.astype(f32) + (1.0 - beta_one) * gradient
    second = beta_two * moment_two.astype(f32) + (1.0 - beta_two) * gradient * gradient
    update = first / corr_one / (jnp.sqrt(second / corr_two) + epsilon)
    return master - learn_rate * (update + weight_decay * master)


def iota(shape, dim):
    return lax.broadcasted_iota(jnp.int32, shape, dim)


def dot(a, b):
    return jnp.dot(a, b, preferred_element_type=f32)


def pack_kernel(count, groups, ids_ref, gates_ref, tok_ref, cot_ref, rows_ref, scaled_ref):
    held, choices = ids_ref.shape
    slots = count * CAP
    eye = (iota((held, held), 0) == iota((held, held), 1)).astype(bf16)
    ids = lax.dot_general(
        ids_ref[...].astype(f32).astype(bf16), eye, (((0,), (0,)), ((), ())), preferred_element_type=f32
    )
    named = [
        (ids[k : k + 1, :] == iota((count, held), 0).astype(f32)).astype(bf16) for k in range(choices)
    ]
    before = (iota((held, held), 0) < iota((held, held), 1)).astype(bf16)
    position = dot(functools.reduce(lambda a, b: a + b, named), before)
    spread = (iota((slots, count), 0) // CAP == iota((slots, count), 1)).astype(bf16)
    slot = (iota((slots, held), 0) % CAP).astype(f32)
    here = dot(spread, position.astype(bf16)) == slot
    places = [jnp.where(here, dot(spread, n), 0.0).astype(bf16) for n in named]
    rows_ref[...] = dot(functools.reduce(lambda a, b: a + b, places), tok_ref[...]).astype(bf16)
    cot = cot_ref[...].astype(f32)
    gates = gates_ref[...]
    scaled = functools.reduce(
        lambda a, b: a + b,
        [dot(places[k], (cot * gates[:, k : k + 1]).astype(bf16)) for k in range(choices)],
    ).astype(bf16)
    width = scaled.shape[1] // groups
    for g in range(groups):
        scaled_ref[g] = scaled[:, g * width : (g + 1) * width]


def hidden_kernel(pieces, *refs):
    up_ref, out_ref = refs[pieces], refs[pieces + 1]
    rows = jnp.concatenate([r[...] for r in refs[:pieces]], axis=0)
    u = dot(rows, up_ref[0])
    out_ref[...] = (u / (1.0 + jnp.exp(-u))).T.astype(bf16)


def step_of(power, mantissa):
    return mantissa * jnp.exp2(power) * (1.0 / TOP)


def adam_kernel(count, me_ref, *refs):
    hid = refs[:count]
    scaled_ref, master_ref, one_ref, two_ref = refs[count : count + 4]
    outs = refs[len(refs) - count :]
    j = pl.program_id(0)
    rows, width = master_ref.shape[1:]
    lanes = width // LANES

    def fresh(k):
        gradient = dot(hid[k][...], scaled_ref[0])
        return adam_update(master_ref[0], one_ref[0], two_ref[0], gradient)

    @pl.when(j == 0)
    def _():
        outs[0][0] = fresh(0)

    for k in range(1, count):

        @pl.when(j == k)
        def _(k=k):
            new = fresh(k)
            most = jnp.maximum(jnp.max(jnp.abs(new), axis=0, keepdims=True), FLOOR)
            power = jnp.floor(jnp.log2(most)) - 13.0
            mantissa = jnp.floor(most * jnp.exp2(-power)) + 2.0
            inverse = 1.0 / step_of(power, mantissa)
            code = jnp.round(new * inverse).astype(jnp.int32).astype(jnp.int16)
            extra = outs[k].shape[0] - rows * lanes
            row = iota((extra, LANES), 0)
            scale = jnp.zeros((extra, LANES), f32)
            for t in range(lanes):
                at = slice(t * LANES, (t + 1) * LANES)
                outs[k][t * rows : (t + 1) * rows, :] = code[:, at]
                scale = jnp.where(row == 2 * t, power[:, at], scale)
                scale = jnp.where(row == 2 * t + 1, mantissa[:, at], scale)
            outs[k][lanes * rows :, :] = scale.astype(jnp.int32).astype(jnp.int16)


def place_kernel(count, me_ref, *refs):
    codes, out_ref = refs[: count - 1], refs[-1]
    j = pl.program_id(0)
    rows, width = out_ref.shape[1:]
    lanes = width // LANES
    for k in range(1, count):

        @pl.when(j == k - 1)
        def _(k=k):
            code = codes[k - 1]
            scale = code[lanes * rows :, :].astype(jnp.int32).astype(f32)
            for t in range(lanes):
                step = step_of(scale[2 * t : 2 * t + 1, :], scale[2 * t + 1 : 2 * t + 2, :])
                out_ref[0, :, t * LANES : (t + 1) * LANES] = (
                    code[t * rows : (t + 1) * rows, :].astype(jnp.int32).astype(f32) * step
                )


def swap(x, axis, size, k):
    return lax.ppermute(x, axis, [(i, i ^ k) for i in range(size)])


def gathered(x, size):
    near = [x if k == 0 else swap(x, "dp", size, k) for k in range(0, size, 2)]
    far = [swap(b, "dp", size, 1) for b in near]
    return near + far


def body(sizes, tokens, cotangent, experts, gate_weights, w_up, master, moment_one, moment_two):
    count, size = sizes
    me = lax.axis_index("expert").astype(jnp.int32)[None]
    held, model = tokens.shape
    units = w_up.shape[2]
    width = master.shape[2]
    assert master.shape[0] == count and count & (count - 1) == 0 and size & (size - 1) == 0
    slots = count * CAP

    rows, scaled = pl.pallas_call(
        functools.partial(pack_kernel, count, count),
        out_shape=(
            jax.ShapeDtypeStruct((slots, model), bf16),
            jax.ShapeDtypeStruct((count, slots, width), bf16),
        ),
        in_specs=[VMEM] * 4,
        out_specs=(VMEM, VMEM),
        name="pack",
    )(experts, gate_weights, tokens, cotangent)
    got_rows = lax.all_to_all(rows.reshape(count, CAP, model), "expert", 0, 0, tiled=True)
    got_scaled = lax.all_to_all(scaled, "expert", 0, 0, tiled=True)
    all_rows = gathered(got_rows.reshape(slots, model), size)
    all_scaled = gathered(got_scaled.reshape(slots * count, width), size)
    total = size * slots
    scaled_of = (
        jnp.stack(all_scaled)
        .reshape(size, count, count, CAP, width)
        .transpose(2, 0, 1, 3, 4)
        .reshape(count, total, width)
    )

    chunk = max(LANES, units // 4)
    chunks = units // chunk
    hidden = []
    for i in range(chunks):
        own = pl.pallas_call(
            functools.partial(hidden_kernel, size),
            grid=(1,),
            out_shape=jax.ShapeDtypeStruct((chunk, total), bf16),
            in_specs=[pl.BlockSpec((slots, model), lambda g: (0, 0))] * size
            + [pl.BlockSpec((1, model, chunk), lambda g, i=i: (0, 0, i))],
            out_specs=pl.BlockSpec((chunk, total), lambda g: (0, 0)),
            cost_estimate=pl.CostEstimate(
                flops=2 * total * model * chunk, bytes_accessed=2 * model * (chunk + total), transcendentals=total * chunk
            ),
            name=f"hidden_{i}",
        )(*all_rows, w_up)
        hidden.append([own] + [swap(own, "expert", count, k) for k in range(1, count)])

    lanes = width // LANES
    extra = -(-2 * lanes // TILE) * TILE
    packed = (lanes * chunk + extra, LANES)
    out = None
    arrived = []
    for i in range(chunks):
        whole = lambda j, me: (0, 0)
        part = lambda j, me, i=i: (me[0] ^ j, i, 0)
        aliased = [] if out is None else [out]
        results = pl.pallas_call(
            functools.partial(adam_kernel, count),
            grid_spec=pltpu.PrefetchScalarGridSpec(
                num_scalar_prefetch=1,
                grid=(count,),
                in_specs=[pl.BlockSpec((chunk, total), whole)] * count
                + [pl.BlockSpec((1, total, width), lambda j, me: (me[0] ^ j, 0, 0))]
                + [pl.BlockSpec((1, chunk, width), part)] * 3
                + [pl.BlockSpec(memory_space=pl.ANY)] * len(aliased),
                out_specs=[pl.BlockSpec((1, chunk, width), lambda j, me, i=i: (0, i, me[0]))]
                + [pl.BlockSpec(packed, whole)] * (count - 1),
            ),
            out_shape=[jax.ShapeDtypeStruct((1, units, model), f32)]
            + [jax.ShapeDtypeStruct(packed, jnp.int16)] * (count - 1),
            input_output_aliases={count + 5: 0} if aliased else {},
            cost_estimate=pl.CostEstimate(
                flops=2 * total * width * chunk * count, bytes_accessed=12 * count * chunk * width, transcendentals=0
            ),
            name=f"adam_{i}",
        )(me, *hidden[i], scaled_of, master, moment_one, moment_two, *aliased)
        out = results[0]
        arrived.append([swap(results[k], "expert", count, k) for k in range(1, count)])
    for i in range(chunks):
        out = pl.pallas_call(
            functools.partial(place_kernel, count),
            grid_spec=pltpu.PrefetchScalarGridSpec(
                num_scalar_prefetch=1,
                grid=(count - 1,),
                in_specs=[pl.BlockSpec(packed, lambda j, me: (0, 0))] * (count - 1)
                + [pl.BlockSpec(memory_space=pl.ANY)],
                out_specs=pl.BlockSpec((1, chunk, width), lambda j, me, i=i: (0, i, me[0] ^ (j + 1))),
            ),
            out_shape=jax.ShapeDtypeStruct((1, units, model), f32),
            input_output_aliases={count: 0},
            cost_estimate=pl.CostEstimate(flops=0, bytes_accessed=6 * (count - 1) * chunk * width, transcendentals=0),
            name=f"place_{i}",
        )(me, *arrived[i], out)
    return out


def solution(mesh):
    placed = (
        P(("expert", "dp"), None),
        P(("expert", "dp"), None),
        P(("expert", "dp"), None),
        P(("expert", "dp"), None),
        P("expert", None, "dp"),
        P(None, "dp", "expert"),
        P(None, "dp", "expert"),
        P(None, "dp", "expert"),
    )
    sizes = (mesh.shape["expert"], mesh.shape["dp"])
    return jax.shard_map(
        functools.partial(body, sizes),
        mesh=mesh,
        in_specs=placed,
        out_specs=P("expert", "dp", None),
        check_vma=False,
    )
```
